32 devices in a mesh: groups: 2 (over y), ctx: 4 (over z), head: 2 (over x), sub: 2 (over core).
Axes of the slice: x: 2, y: 2, z: 4, core: 2. Of those that a mesh axis runs over, the one named last changes fastest.
Arguments:
- queries: bfloat16 [4096, 8, 8, 128], P(('groups', 'ctx'), 'head', 'sub'), parts along dimension 0, may hold values from -6 to 6
- keys: bfloat16 [4096, 8, 128], P(('groups', 'ctx'), ('head', 'sub')), parts along dimension 0, may hold values from -6 to 6
- values: bfloat16 [4096, 8, 128], P(('groups', 'ctx'), ('head', 'sub')), parts along dimension 0, may hold values from -6 to 6
- span_order: int32 [8], replicated, may hold values from 0 to 7, as said below
Outputs:
- attended: bfloat16 [4096, 8, 8, 128], P(('groups', 'ctx'), 'head', 'sub'), parts along dimension 0
The draws below stay inside these ranges and needn't reach their ends.
There are 2 independent parts, one for each index of `groups`. The reference program is written for one: setup_inputs(seed, part) draws one part's arguments, and reference() takes and returns one part's arrays. A program takes and returns all parts, laid end to end along the dimension named above; an argument that names none is the same for every part. Nothing has to cross between parts.
Inputs may be any that keep to these rules, and one draw needn't show every extreme that they name: `span_order`: each block index appears exactly once, and for every i the stored blocks 2 i and 2 i + 1 hold block indices that sum to 7.
All inputs are finite; a program needn't handle non-finite values.
Results may differ from the reference program's by a relative error of at most 0.0049.
Values may be sent and summed in bfloat16 or wider, within the bound.
A program may use at most 64 MiB of HBM per device.

```python
import math
import jax
import jax.numpy as jnp
from jax import lax

KEY_VALUE_HEADS = 8
QUERIES_PER_KV = 8
HEAD_SIZE = 128
SPAN = 256
SEQUENCE_TOKENS = 2048


def drawn_pair(key):
    query_random_seed = jax.random.fold_in(key, 11)
    key_random_seed = jax.random.fold_in(key, 12)
    sampled_queries = jnp.clip(jax.random.normal(query_random_seed, (SEQUENCE_TOKENS, KEY_VALUE_HEADS, QUERIES_PER_KV, HEAD_SIZE), jnp.float32), -6.0, 6.0)
    sampled_keys = jnp.clip(jax.random.normal(key_random_seed, (SEQUENCE_TOKENS, KEY_VALUE_HEADS, HEAD_SIZE), jnp.float32), -6.0, 6.0)
    return (sampled_queries.astype(jnp.bfloat16), sampled_keys.astype(jnp.bfloat16))


def draw_queries(key, part):
    return drawn_pair(key)[0]


def draw_keys(key, part):
    return drawn_pair(key)[1]


def draw_span_order(key, part):
    cycle_count = SEQUENCE_TOKENS // SPAN // 2
    order_key = jax.random.fold_in(key, 21)
    lower = jax.random.permutation(order_key, cycle_count).astype(jnp.int32)
    upper = (2 * cycle_count - 1 - lower).astype(jnp.int32)
    return jnp.stack((lower, upper), axis=1).reshape(-1).astype(jnp.int32)


def shard_levels(own_key, shape, pieces, smallest, top_value):
    level = 1.0
    for position, shards_of in pieces:
        draws = jax.random.uniform(jax.random.fold_in(jax.random.fold_in(own_key, 6), position), (shards_of,), jnp.float32, smallest / len(pieces), top_value / len(pieces))
        level = level * jnp.repeat(jnp.exp(draws), shape[position] // shards_of).reshape((-1,) + (1,) * (len(shape) - 1 - position))
    return level


def normal_values(stream_key, dims, spread, bound, split=(), kind=jnp.bfloat16):
    entries = jax.random.normal(stream_key, dims, jnp.float32) * spread
    if len(split) > 0:
        entries = shard_levels(stream_key, dims, split, -0.22, 0.18) * entries
    return jnp.clip(entries, min=-bound, max=bound).astype(kind)


def setup_inputs(seed: int = 0, part: int = 0) -> dict:
    streams_of = jax.random.split(jax.random.key(seed), 5)
    part_splits = jax.random.split(jax.random.fold_in(streams_of[4], part), 5)
    queries = draw_queries(jax.random.fold_in(jax.random.fold_in(streams_of[4], part), 71), part)
    keys = draw_keys(jax.random.fold_in(jax.random.fold_in(streams_of[4], part), 71), part)
    values = normal_values(part_splits[2], (SEQUENCE_TOKENS, KEY_VALUE_HEADS, HEAD_SIZE), 1.0, 6.0, ((0, 4), (1, 4)))
    span_order = draw_span_order(jax.random.fold_in(streams_of[4], 71), part)
    return {"queries": queries, "keys": keys, "values": values, "span_order": span_order}


def reference(queries, keys, values, span_order):
    offsets = jnp.arange(SPAN, dtype=jnp.int32)
    positions = (span_order[:, None] * SPAN + offsets[None, :]).reshape(-1).astype(jnp.int32)
    scale = 1.0 / math.sqrt(HEAD_SIZE)
    sequence_blocks = SEQUENCE_TOKENS // SPAN

    def single_head(head_index):
        key_rows = keys[:, head_index, :].astype(jnp.float32)
        value_rows = values[:, head_index, :].astype(jnp.float32)
        query_rows = queries[:, head_index].reshape(sequence_blocks, SPAN, QUERIES_PER_KV, HEAD_SIZE)
        query_pos = positions.reshape(sequence_blocks, SPAN)

        def one_block(inputs):
            query_block, block_pos = inputs
            scores = jnp.einsum('rqd,kd->qrk', query_block.astype(jnp.float32), key_rows, precision=lax.Precision.HIGHEST) * scale
            visible = positions[None, None, :] <= block_pos[None, :, None]
            scores = jnp.where(visible, scores, -1e+30)
            peak = lax.optimization_barrier(jnp.max(scores, axis=-1, keepdims=True))
            weights = jnp.where(visible, jnp.exp(scores - peak), 0.0)
            total = lax.optimization_barrier(jnp.sum(weights, axis=-1))
            rounded = lax.optimization_barrier(weights.astype(jnp.bfloat16)).astype(jnp.float32)
            summed = jnp.einsum('qrk,kd->rqd', rounded, value_rows, precision=lax.Precision.HIGHEST)
            return (summed / jnp.transpose(total)[:, :, None]).astype(jnp.bfloat16)
        result = lax.map(one_block, (query_rows, query_pos))
        return result.reshape(SEQUENCE_TOKENS, QUERIES_PER_KV, HEAD_SIZE)
    stacked_heads = lax.map(single_head, jnp.arange(KEY_VALUE_HEADS, dtype=jnp.int32))
    return jnp.transpose(stacked_heads, (1, 0, 2, 3))
```

```python
import functools
import math

import jax
import jax.numpy as jnp
from jax import lax
from jax.experimental import pallas as pl
from jax.experimental.pallas import tpu as pltpu
from jax.sharding import PartitionSpec as P

MESH = pl.DeviceIdType.MESH
HIDDEN = -1e30


def scores_of(q, k):
    return lax.dot_general(q, k, (((1,), (1,)), ((), ())), preferred_element_type=jnp.float32)


def kernel(
    n, span_ref, q_any, k_any, v_any, out_any, raw, q_raw, q_ref, o_ref, buf, acc, peak, total, weights, rescale,
    send_sem, recv_sem, pair_send, pair_recv, own_sem, q_sem, o_sem
):
    z = lax.axis_index("ctx")
    c = lax.axis_index("sub")
    rows, heads, width = k_any.shape
    parts = 2
    groups = 2 * heads
    span = rows // 2
    per_row = q_any.shape[2]
    factor = math.log2(math.e) / math.sqrt(width)
    has_left, has_right = z > 0, z < n - 1

    def to_left(src, block, h, p):
        return pltpu.make_async_remote_copy(
            src_ref=src, dst_ref=buf.at[0, block, h, p], send_sem=send_sem.at[0, block, h, p],
            recv_sem=recv_sem.at[block, h, p], device_id={"ctx": z - 1}, device_id_type=MESH)

    def to_right(src, block, h, p):
        return pltpu.make_async_remote_copy(
            src_ref=src, dst_ref=buf.at[0, block, h, p], send_sem=send_sem.at[1, block, h, p],
            recv_sem=recv_sem.at[block, h, p], device_id={"ctx": z + 1}, device_id_type=MESH)

    def to_pair(src, block, h, p):
        return pltpu.make_async_remote_copy(
            src_ref=src, dst_ref=buf.at[1, block, h, p], send_sem=pair_send.at[block, h, p],
            recv_sem=pair_recv.at[block, h, p], device_id={"sub": 1 - c}, device_id_type=MESH)

    def own_copy(p):
        return pltpu.make_async_copy((k_any, v_any)[p], raw.at[p], own_sem.at[p])

    def q_copy(g):
        return pltpu.make_async_copy(q_any.at[:, g], q_raw.at[g], q_sem.at[g])

    def o_copy(g):
        return pltpu.make_async_copy(o_ref.at[g], out_any.at[:, g], o_sem.at[g])

    for p in range(parts):
        own_copy(p).start()

    barrier = pltpu.get_barrier_semaphore()
    pl.semaphore_signal(barrier, inc=1, device_id={"sub": 1 - c}, device_id_type=MESH)

    @pl.when(has_left)
    def _():
        pl.semaphore_signal(barrier, inc=1, device_id={"ctx": z - 1}, device_id_type=MESH)

    @pl.when(has_right)
    def _():
        pl.semaphore_signal(barrier, inc=1, device_id={"ctx": z + 1}, device_id_type=MESH)

    for g in range(groups):
        q_copy(g).start()

    my_first, my_second = span_ref[2 * z], span_ref[2 * z + 1]
    my_low = jnp.minimum(my_first, my_second)
    flipped = my_first > my_second

    def in_order(first, second):
        return jnp.where(flipped, second, first), jnp.where(flipped, first, second)

    for p in range(parts):
        own_copy(p).wait()
    for p in range(parts):
        stored = jnp.swapaxes(raw[p], 0, 1)
        for h in range(heads):
            for half, picked in enumerate(in_order(stored[h, :span], stored[h, span:])):
                buf[0, z, h, p, half] = picked

    pl.semaphore_wait(barrier, 1 + jnp.where(has_left, 1, 0) + jnp.where(has_right, 1, 0))

    for h in range(heads):
        for p in range(parts):
            src = buf.at[0, z, h, p]

            @pl.when(has_left)
            def _(src=src, h=h, p=p):
                to_left(src, z, h, p).start()

            @pl.when(has_right)
            def _(src=src, h=h, p=p):
                to_right(src, z, h, p).start()

            to_pair(src, z, h, p).start()

    def weigh(scores, top):
        return jnp.exp2((scores - top) * factor)

    def row_max(s):
        return jnp.max(s, axis=0, keepdims=True)

    def row_sum(s):
        return jnp.sum(s, axis=0, keepdims=True)

    def mix(w, v):
        return lax.dot_general(
            v, w.astype(jnp.bfloat16), (((0,), (0,)), ((), ())), preferred_element_type=jnp.float32)

    def load_queries(g):
        first = q_raw[g, :span].reshape(per_row, span, width)
        second = q_raw[g, span:].reshape(per_row, span, width)
        for half, picked in enumerate(in_order(first, second)):
            q_ref[g, half] = picked

    def finish(g):
        low = (acc[0, g] * (1.0 / total[0, g])).astype(jnp.bfloat16)
        high = (acc[1, g] * (1.0 / total[1, g])).astype(jnp.bfloat16)
        first, second = jnp.where(flipped, high, low), jnp.where(flipped, low, high)
        for i, rows_of in enumerate((first, second)):
            o_ref[g, i * span : (i + 1) * span] = rows_of.T.reshape(span, per_row, width)
        o_copy(g).start()

    def own_head(k, v, g):
        load_queries(g)
        k_at = lax.broadcasted_iota(jnp.int32, (span, span), 0)
        q_at = lax.broadcasted_iota(jnp.int32, (span, span), 1)
        for j in range(per_row):
            cols = slice(j * span, (j + 1) * span)
            visible = k_at <= (q_at + j * span) // per_row
            q_low, q_high = q_ref[g, 0, j], q_ref[g, 1, j]
            s = jnp.where(visible, scores_of(k[0], q_low), HIDDEN)
            top = row_max(s)
            w = weigh(s, top)
            peak[0, g, :, cols] = top
            total[0, g, :, cols] = row_sum(w)
            acc[0, g, :, cols] = mix(w, v[0])
            s1 = scores_of(k[0], q_high)
            s2 = jnp.where(visible, scores_of(k[1], q_high), HIDDEN)
            top = jnp.maximum(row_max(s1), row_max(s2))
            w1, w2 = weigh(s1, top), weigh(s2, top)
            peak[1, g, :, cols] = top
            total[1, g, :, cols] = row_sum(w1) + row_sum(w2)
            acc[1, g, :, cols] = mix(w1, v[0]) + mix(w2, v[1])

    def below_of(block):
        return jnp.minimum(span_ref[2 * block], span_ref[2 * block + 1]) < my_low

    def other_weights(k, block, g, slot):
        below = below_of(block)
        k_low, k_pick = k[0], jnp.where(below, k[0], k[1])
        for j in range(per_row):
            cols = slice(j * span, (j + 1) * span)
            s1 = scores_of(k_low, q_ref[g, 1, j])
            s2 = scores_of(k_pick, jnp.where(below, q_ref[g, 0, j], q_ref[g, 1, j]))
            top1, top2 = row_max(s1), row_max(s2)
            old_low, old_high = peak[0, g, :, cols], peak[1, g, :, cols]
            new_low = jnp.where(below, jnp.maximum(old_low, top2), old_low)
            new_high = jnp.maximum(old_high, jnp.where(below, top1, jnp.maximum(top1, top2)))
            w1 = weigh(s1, new_high)
            w2 = weigh(s2, jnp.where(below, new_low, new_high))
            sum1, sum2 = row_sum(w1), row_sum(w2)
            weights[slot, 0, :, cols] = w1.astype(jnp.bfloat16)
            weights[slot, 1, :, cols] = w2.astype(jnp.bfloat16)
            r_low, r_high = weigh(old_low, new_low), weigh(old_high, new_high)
            peak[0, g, :, cols] = new_low
            peak[1, g, :, cols] = new_high
            total[0, g, :, cols] = total[0, g, :, cols] * r_low + jnp.where(below, sum2, 0.0)
            total[1, g, :, cols] = total[1, g, :, cols] * r_high + jnp.where(below, sum1, sum1 + sum2)
            rescale[slot, 0, :, cols] = r_low
            rescale[slot, 1, :, cols] = r_high

    def other_values(v, block, g, slot):
        below = below_of(block)
        v_low, v_pick = v[0], jnp.where(below, v[0], v[1])
        for j in range(per_row):
            cols = slice(j * span, (j + 1) * span)
            o1, o2 = mix(weights[slot, 0, :, cols], v_low), mix(weights[slot, 1, :, cols], v_pick)
            r_low, r_high = rescale[slot, 0, :, cols], rescale[slot, 1, :, cols]
            acc[0, g, :, cols] = acc[0, g, :, cols] * r_low + jnp.where(below, o2, 0.0)
            acc[1, g, :, cols] = acc[1, g, :, cols] * r_high + jnp.where(below, o1, o1 + o2)

    for g in range(groups):
        q_copy(g).wait()

    def own_step(h, carry):
        own_head(buf[0, z, h, 0], buf[0, z, h, 1], c * heads + h)
        return carry

    lax.fori_loop(0, heads, own_step, 0)

    def pair_step(h, carry):
        for p in range(parts):
            to_pair(buf.at[0, z, h, p], z, h, p).wait_recv()
        own_head(buf[1, z, h, 0], buf[1, z, h, 1], (1 - c) * heads + h)
        return carry

    lax.fori_loop(0, heads, pair_step, 0)

    def step(index, carry):
        hop = index // heads + 1
        h = index % heads
        left_block, right_block = z - hop, z + hop

        def relay(p):
            @pl.when(left_block >= 0)
            def _():
                block = left_block
                src = buf.at[0, block, h, p]
                to_right(src, block, h, p).wait_recv()

                @pl.when(has_right)
                def _():
                    to_right(src, block, h, p).start()

                to_pair(src, block, h, p).start()

            @pl.when(right_block < n)
            def _():
                block = right_block
                src = buf.at[0, block, h, p]
                to_left(src, block, h, p).wait_recv()

                @pl.when(has_left)
                def _():
                    to_left(src, block, h, p).start()

                to_pair(src, block, h, p).start()

        def part(p, use, which, carry):
            side = which // 2
            block = jnp.where(which % 2 == 0, left_block, right_block)
            g = jnp.where(side == 0, c, 1 - c) * heads + h

            @pl.when((block >= 0) & (block < n))
            def _():
                @pl.when(side == 1)
                def _():
                    to_pair(buf.at[0, block, h, p], block, h, p).wait_recv()

                use(buf[side, block, h, p], block, g, which)

            if p == 1:
                @pl.when((hop == n - 1) & (which % 2 == 1))
                def _():
                    finish(g)

            return carry

        relay(0)
        lax.fori_loop(0, 4, functools.partial(part, 0, other_weights), 0)
        relay(1)
        return lax.fori_loop(0, 4, functools.partial(part, 1, other_values), carry)

    lax.fori_loop(0, (n - 1) * heads, step, 0)

    def drain(index, carry):
        block = index // heads
        h = index % heads
        for p in range(parts):
            src = buf.at[0, block, h, p]

            @pl.when(has_left & (block >= z))
            def _(src=src, p=p):
                to_left(src, block, h, p).wait_send()

            @pl.when(has_right & (block <= z))
            def _(src=src, p=p):
                to_right(src, block, h, p).wait_send()

            to_pair(src, block, h, p).wait_send()
        return carry

    lax.fori_loop(0, n * heads, drain, 0)
    for g in range(groups):
        o_copy(g).wait()


def on_device(n, queries, keys, values, span_order):
    rows, groups, per_group, width = queries.shape
    heads = keys.shape[1]
    span = rows // 2
    q_rows = span * per_group
    in_hbm = pl.BlockSpec(memory_space=pltpu.HBM)
    return pl.pallas_call(
        functools.partial(kernel, n),
        out_shape=jax.ShapeDtypeStruct(queries.shape, jnp.bfloat16),
        in_specs=[pl.BlockSpec(memory_space=pltpu.SMEM), in_hbm, in_hbm, in_hbm],
        out_specs=pl.BlockSpec(memory_space=pl.ANY),
        scratch_shapes=[
            pltpu.VMEM((2, rows, heads, width), jnp.bfloat16),
            pltpu.VMEM((groups, rows, per_group, width), jnp.bfloat16),
            pltpu.VMEM((groups, 2, per_group, span, width), jnp.bfloat16),
            pltpu.VMEM((groups, rows, per_group, width), jnp.bfloat16),
            pltpu.VMEM((2, n, heads, 2, 2, span, width), jnp.bfloat16),
            pltpu.VMEM((2, groups, width, q_rows), jnp.float32),
            pltpu.VMEM((2, groups, 1, q_rows), jnp.float32),
            pltpu.VMEM((2, groups, 1, q_rows), jnp.float32),
            pltpu.VMEM((4, 2, span, q_rows), jnp.bfloat16),
            pltpu.VMEM((4, 2, 1, q_rows), jnp.float32),
            pltpu.SemaphoreType.DMA((2, n, heads, 2)),
            pltpu.SemaphoreType.DMA((n, heads, 2)),
            pltpu.SemaphoreType.DMA((n, heads, 2)),
            pltpu.SemaphoreType.DMA((n, heads, 2)),
            pltpu.SemaphoreType.DMA((2,)),
            pltpu.SemaphoreType.DMA((groups,)),
            pltpu.SemaphoreType.DMA((groups,)),
        ],
        compiler_params=pltpu.CompilerParams(
            collective_id=0, has_side_effects=True, vmem_limit_bytes=48 * 1024 * 1024),
    )(*(pltpu.with_memory_space_constraint(a, pltpu.HBM) for a in (span_order, queries, keys, values)))


def solution(mesh):
    return jax.shard_map(
        functools.partial(on_device, mesh.shape["ctx"]),
        mesh=mesh,
        in_specs=(
            P(("groups", "ctx"), "head", "sub", None),
            P(("groups", "ctx"), ("head", "sub"), None),
            P(("groups", "ctx"), ("head", "sub"), None),
            P(),
        ),
        out_specs=P(("groups", "ctx"), "head", "sub", None),
        check_vma=False,
    )
```

```python
import functools
import math

import jax
import jax.numpy as jnp
from jax import lax
from jax.experimental import pallas as pl
from jax.experimental.pallas import tpu as pltpu
from jax.sharding import PartitionSpec as P

MESH = pl.DeviceIdType.MESH
HIDDEN = -1e30
MOST_LAYOUTS = 4


def scores_of(q, k):
    return lax.dot_general(q, k, (((1,), (1,)), ((), ())), preferred_element_type=jnp.float32)


def kernel(
    n, inner, span_ref, q_any, k_any, v_any, out_ref, raw, q_raw, q_ref, buf, acc, peak, total, weights, rescale,
    send_sem, recv_sem, pair_send, pair_recv, own_sem, q_sem
):
    z = lax.axis_index("ctx")
    c = lax.axis_index("sub")
    rows, heads, width = k_any.shape
    parts = 2
    groups = 2 * heads
    span = rows // 2
    per_row = q_any.shape[2]
    factor = math.log2(math.e) / math.sqrt(width)
    has_left, has_right = z > 0, z < n - 1

    def seen_ahead(block, ahead):
        if not inner:
            return None
        wide = block != inner[0]
        return wide & ((block != inner[1]) | ahead) if len(inner) > 1 else wide

    def pick_size(wide, copy, act):
        if wide is None:
            act(copy(True))
            return

        @pl.when(wide)
        def _():
            act(copy(True))

        @pl.when(jnp.logical_not(wide))
        def _():
            act(copy(False))

    def block_of(side, block, h, p, wide):
        whole = buf.at[side, block, h, p]
        return whole if wide else whole.at[0]

    def left(block, h, p, act, at=0):
        def copy(wide):
            part = block_of(0, block, h, p, wide)
            return pltpu.make_async_remote_copy(
                src_ref=part, dst_ref=part, send_sem=send_sem.at[0, block, h, p],
                recv_sem=recv_sem.at[block, h, p], device_id={"ctx": z - 1}, device_id_type=MESH)

        pick_size(seen_ahead(block, inner[0] <= z - 1 + at) if inner else None, copy, act)

    def right(block, h, p, act, at=0):
        def copy(wide):
            part = block_of(0, block, h, p, wide)
            return pltpu.make_async_remote_copy(
                src_ref=part, dst_ref=part, send_sem=send_sem.at[1, block, h, p],
                recv_sem=recv_sem.at[block, h, p], device_id={"ctx": z + 1}, device_id_type=MESH)

        pick_size(seen_ahead(block, inner[0] >= z + 1 - at) if inner else None, copy, act)

    def pair(block, h, p, act):
        def copy(wide):
            return pltpu.make_async_remote_copy(
                src_ref=block_of(0, block, h, p, wide), dst_ref=block_of(1, block, h, p, wide),
                send_sem=pair_send.at[block, h, p], recv_sem=pair_recv.at[block, h, p],
                device_id={"sub": 1 - c}, device_id_type=MESH)

        pick_size((block == z) | seen_ahead(block, inner[0] == z) if inner else None, copy, act)

    def start(copy):
        copy.start()

    def sent(copy):
        copy.wait_send()

    def arrived(copy):
        copy.wait_recv()

    def own_copy(p):
        return pltpu.make_async_copy((k_any, v_any)[p], raw.at[p], own_sem.at[p])

    def q_copy(g):
        return pltpu.make_async_copy(q_any.at[:, g], q_raw.at[g], q_sem.at[g])

    for p in range(parts):
        own_copy(p).start()

    barrier = pltpu.get_barrier_semaphore()
    pl.semaphore_signal(barrier, inc=1, device_id={"sub": 1 - c}, device_id_type=MESH)

    @pl.when(has_left)
    def _():
        pl.semaphore_signal(barrier, inc=1, device_id={"ctx": z - 1}, device_id_type=MESH)

    @pl.when(has_right)
    def _():
        pl.semaphore_signal(barrier, inc=1, device_id={"ctx": z + 1}, device_id_type=MESH)

    for g in range(groups):
        q_copy(g).start()

    my_first, my_second = span_ref[2 * z], span_ref[2 * z + 1]
    my_low = jnp.minimum(my_first, my_second)
    flipped = my_first > my_second

    def in_order(first, second):
        return jnp.where(flipped, second, first), jnp.where(flipped, first, second)

    for p in range(parts):
        own_copy(p).wait()
        stored = jnp.swapaxes(raw[p], 0, 1)
        for h in range(heads):
            for half, picked in enumerate(in_order(stored[h, :span], stored[h, span:])):
                buf[0, z, h, p, half] = picked
        if p == 0:
            pl.semaphore_wait(barrier, 1 + jnp.where(has_left, 1, 0) + jnp.where(has_right, 1, 0))
        for h, which in [(0, 0)] if p == 0 else [(h, q) for h in range(heads) for q in range(parts)][1:]:
            @pl.when(has_left)
            def _(h=h, which=which):
                left(z, h, which, start)

            @pl.when(has_right)
            def _(h=h, which=which):
                right(z, h, which, start)

            pair(z, h, which, start)

    def weigh(scores, top):
        return jnp.exp2((scores - top) * factor)

    def row_max(s):
        return jnp.max(s, axis=0, keepdims=True)

    def with_ones(v):
        return jnp.concatenate([v.T, jnp.ones((16, span), jnp.bfloat16)], axis=0)

    def mix(w, v):
        r = lax.dot_general(v, w, (((1,), (0,)), ((), ())), preferred_element_type=jnp.float32)
        return r[:width], r[width : width + 1]

    def in_stages(score, soften, gather):
        s = score(0)
        held = None
        for j in range(per_row):
            now, s = s, score(j + 1) if j + 1 < per_row else None
            if held is not None:
                gather(j - 1, *held)
            held = soften(j, *now)
        gather(per_row - 1, *held)

    def load_queries(g):
        first = q_raw[g, :span].reshape(per_row, span, width)
        second = q_raw[g, span:].reshape(per_row, span, width)
        for half, picked in enumerate(in_order(first, second)):
            q_ref[g, half] = picked

    def finish(g):
        low = (acc[0, g] * (1.0 / total[0, g])).astype(jnp.bfloat16)
        high = (acc[1, g] * (1.0 / total[1, g])).astype(jnp.bfloat16)
        first, second = jnp.where(flipped, high, low), jnp.where(flipped, low, high)
        for i, rows_of in enumerate((first, second)):
            out_ref[i * span : (i + 1) * span, g] = rows_of.T.reshape(span, per_row, width)

    def own_head(k, v, g):
        load_queries(g)
        k_at = lax.broadcasted_iota(jnp.int32, (span, span), 0)
        q_at = lax.broadcasted_iota(jnp.int32, (span, span), 1)
        v_low, v_high = with_ones(v[0]), with_ones(v[1])

        def score(j):
            return scores_of(k[0], q_ref[g, 0, j]), scores_of(k[0], q_ref[g, 1, j]), scores_of(k[1], q_ref[g, 1, j])

        def soften(j, s, s1, s2):
            cols = slice(j * span, (j + 1) * span)
            visible = k_at <= (q_at + j * span) // per_row
            s = jnp.where(visible, s, HIDDEN)
            s2 = jnp.where(visible, s2, HIDDEN)
            top = row_max(s)
            w = weigh(s, top).astype(jnp.bfloat16)
            peak[0, g, :, cols] = top
            top = jnp.maximum(row_max(s1), row_max(s2))
            peak[1, g, :, cols] = top
            return w, weigh(s1, top).astype(jnp.bfloat16), weigh(s2, top).astype(jnp.bfloat16)

        def gather(j, w, w1, w2):
            cols = slice(j * span, (j + 1) * span)
            acc[0, g, :, cols], total[0, g, :, cols] = mix(w, v_low)
            o1, sum1 = mix(w1, v_low)
            o2, sum2 = mix(w2, v_high)
            acc[1, g, :, cols] = o1 + o2
            total[1, g, :, cols] = sum1 + sum2

        in_stages(score, soften, gather)

    def below_of(block):
        return jnp.minimum(span_ref[2 * block], span_ref[2 * block + 1]) < my_low

    def other_head(k, v, block, g, slot):
        below = below_of(block)

        def score(j):
            k_low, k_pick = k[0], jnp.where(below, k[0], k[1])
            q_pick = jnp.where(below, q_ref[g, 0, j], q_ref[g, 1, j])
            return scores_of(k_low, q_ref[g, 1, j]), scores_of(k_pick, q_pick)

        def soften(j, s1, s2):
            cols = slice(j * span, (j + 1) * span)
            top1, top2 = row_max(s1), row_max(s2)
            old_low, old_high = peak[0, g, :, cols], peak[1, g, :, cols]
            new_low = jnp.where(below, jnp.maximum(old_low, top2), old_low)
            new_high = jnp.maximum(old_high, jnp.where(below, top1, jnp.maximum(top1, top2)))
            w1 = weigh(s1, new_high).astype(jnp.bfloat16)
            w2 = weigh(s2, jnp.where(below, new_low, new_high)).astype(jnp.bfloat16)
            peak[0, g, :, cols] = new_low
            peak[1, g, :, cols] = new_high
            return w1, w2, weigh(old_low, new_low), weigh(old_high, new_high)

        def hold(j, w1, w2, r_low, r_high):
            cols = slice(j * span, (j + 1) * span)
            weights[slot, 0, :, cols] = w1
            weights[slot, 1, :, cols] = w2
            rescale[slot, 0, :, cols] = r_low
            rescale[slot, 1, :, cols] = r_high

        def gather(j, w1, w2, r_low, r_high):
            cols = slice(j * span, (j + 1) * span)
            o1, sum1 = mix(w1, v_low)
            o2, sum2 = mix(w2, v_pick)
            total[0, g, :, cols] = total[0, g, :, cols] * r_low + jnp.where(below, sum2, 0.0)
            total[1, g, :, cols] = total[1, g, :, cols] * r_high + jnp.where(below, sum1, sum1 + sum2)
            acc[0, g, :, cols] = acc[0, g, :, cols] * r_low + jnp.where(below, o2, 0.0)
            acc[1, g, :, cols] = acc[1, g, :, cols] * r_high + jnp.where(below, o1, o1 + o2)

        if v is None:
            in_stages(score, soften, hold)
            return
        v_low, v_pick = with_ones(v[0]), with_ones(jnp.where(below, v[0], v[1]))
        if k is not None:
            in_stages(score, soften, gather)
            return
        for j in range(per_row):
            cols = slice(j * span, (j + 1) * span)
            gather(j, weights[slot, 0, :, cols], weights[slot, 1, :, cols],
                   rescale[slot, 0, :, cols], rescale[slot, 1, :, cols])

    for g in range(groups):
        q_copy(g).wait()

    def own_step(h, carry):
        own_head(buf[0, z, h, 0], buf[0, z, h, 1], c * heads + h)
        return carry

    lax.fori_loop(0, heads, own_step, 0)

    def pair_step(h, carry):
        for p in range(parts):
            pair(z, h, p, arrived)
        own_head(buf[1, z, h, 0], buf[1, z, h, 1], (1 - c) * heads + h)
        return carry

    lax.fori_loop(0, heads, pair_step, 0)

    def step(merged, index, carry):
        hop = index // heads + 1
        h = index % heads
        left_block, right_block = z - hop, z + hop

        def relay(p):
            @pl.when(left_block >= 0)
            def _():
                block = left_block
                right(block, h, p, arrived, at=1)

                @pl.when(has_right)
                def _():
                    right(block, h, p, start)

                pair(block, h, p, start)

            @pl.when(right_block < n)
            def _():
                block = right_block
                left(block, h, p, arrived, at=1)

                @pl.when(has_left)
                def _():
                    left(block, h, p, start)

                pair(block, h, p, start)

        def part(uses, which, carry):
            side = which // 2
            block = jnp.where(which % 2 == 0, left_block, right_block)
            g = jnp.where(side == 0, c, 1 - c) * heads + h

            @pl.when((block >= 0) & (block < n))
            def _():
                @pl.when(side == 1)
                def _():
                    for p in uses:
                        pair(block, h, p, arrived)

                k, v = (buf[side, block, h, p] if p in uses else None for p in range(parts))
                other_head(k, v, block, g, which)

            if uses == (1,):
                @pl.when(which % 2 == 1)
                def _():
                    finish(g)

            return carry

        if merged:
            relay(0)
            relay(1)
            return lax.fori_loop(0, 4, functools.partial(part, (0, 1)), carry)
        relay(0)
        lax.fori_loop(0, 4, functools.partial(part, (0,)), 0)
        relay(1)
        return lax.fori_loop(0, 4, functools.partial(part, (1,)), carry)

    lax.fori_loop(0, (n - 2) * heads, functools.partial(step, True), 0)
    lax.fori_loop((n - 2) * heads, (n - 1) * heads, functools.partial(step, False), 0)

    def drain(index, carry):
        block = index // heads
        h = index % heads
        for p in range(parts):
            @pl.when(has_left & (block >= z))
            def _(p=p):
                left(block, h, p, sent)

            @pl.when(has_right & (block <= z))
            def _(p=p):
                right(block, h, p, sent)

            pair(block, h, p, sent)
        return carry

    lax.fori_loop(0, n * heads, drain, 0)


def attend(n, inner, number, queries, keys, values, span_order):
    rows, groups, per_group, width = queries.shape
    heads = keys.shape[1]
    span = rows // 2
    q_rows = span * per_group
    in_hbm = pl.BlockSpec(memory_space=pltpu.HBM)
    return pl.pallas_call(
        functools.partial(kernel, n, inner),
        out_shape=jax.ShapeDtypeStruct(queries.shape, jnp.bfloat16),
        in_specs=[pl.BlockSpec(memory_space=pltpu.SMEM), in_hbm, in_hbm, in_hbm],
        out_specs=pl.BlockSpec(memory_space=pltpu.VMEM),
        scratch_shapes=[
            pltpu.VMEM((2, rows, heads, width), jnp.bfloat16),
            pltpu.VMEM((groups, rows, per_group, width), jnp.bfloat16),
            pltpu.VMEM((groups, 2, per_group, span, width), jnp.bfloat16),
            pltpu.VMEM((2, n, heads, 2, 2, span, width), jnp.bfloat16),
            pltpu.VMEM((2, groups, width, q_rows), jnp.float32),
            pltpu.VMEM((2, groups, 1, q_rows), jnp.float32),
            pltpu.VMEM((2, groups, 1, q_rows), jnp.float32),
            pltpu.VMEM((4, 2, span, q_rows), jnp.bfloat16),
            pltpu.VMEM((4, 2, 1, q_rows), jnp.float32),
            pltpu.SemaphoreType.DMA((2, n, heads, 2)),
            pltpu.SemaphoreType.DMA((n, heads, 2)),
            pltpu.SemaphoreType.DMA((n, heads, 2)),
            pltpu.SemaphoreType.DMA((n, heads, 2)),
            pltpu.SemaphoreType.DMA((2,)),
            pltpu.SemaphoreType.DMA((groups,)),
        ],
        compiler_params=pltpu.CompilerParams(
            collective_id=number, has_side_effects=True, vmem_limit_bytes=48 * 1024 * 1024),
    )(*(pltpu.with_memory_space_constraint(a, pltpu.HBM) for a in (span_order, queries, keys, values)))


def on_device(n, queries, keys, values, span_order):
    args = (queries, keys, values, span_order)
    if n > MOST_LAYOUTS:
        return attend(n, (), 0, *args)
    first = lax.shift_right_logical(jnp.argmax(span_order).astype(jnp.int32), 1)
    return lax.switch(first, [functools.partial(attend, n, (i,), i) for i in range(n)], *args)


def solution(mesh):
    return jax.shard_map(
        functools.partial(on_device, mesh.shape["ctx"]),
        mesh=mesh,
        in_specs=(
            P(("groups", "ctx"), "head", "sub", None),
            P(("groups", "ctx"), ("head", "sub"), None),
            P(("groups", "ctx"), ("head", "sub"), None),
            P(),
        ),
        out_specs=P(("groups", "ctx"), "head", "sub", None),
        check_vma=False,
    )
```

```python
import functools
import math

import jax
import jax.numpy as jnp
from jax import lax
from jax.experimental import pallas as pl
from jax.experimental.pallas import tpu as pltpu
from jax.sharding import PartitionSpec as P

MESH = pl.DeviceIdType.MESH
HIDDEN = -1e30
PIECE = 64
MOST_LAYOUTS = 4


def scores_of(q, k):
    return lax.dot_general(q, k, (((1,), (1,)), ((), ())), preferred_element_type=jnp.float32)


def kernel(
    n, inner, span_ref, q_any, k_any, v_any, out_ref, raw, q_raw, q_ref, buf, acc, peak, total, weights, rescale,
    send_sem, recv_sem, pair_send, pair_recv, own_sem, q_sem
):
    z = lax.axis_index("ctx")
    c = lax.axis_index("sub")
    rows, heads, width = k_any.shape
    parts = 2
    groups = 2 * heads
    span = rows // 2
    per_row = q_any.shape[2]
    factor = math.log2(math.e) / math.sqrt(width)
    has_left, has_right = z > 0, z < n - 1

    def seen_ahead(block, ahead):
        if not inner:
            return None
        wide = block != inner[0]
        return wide & ((block != inner[1]) | ahead) if len(inner) > 1 else wide

    def pick_size(wide, copy, act):
        if wide is None:
            act(copy(True))
            return

        @pl.when(wide)
        def _():
            act(copy(True))

        @pl.when(jnp.logical_not(wide))
        def _():
            act(copy(False))

    def block_of(side, block, h, p, wide):
        whole = buf.at[side, block, h, p]
        return whole if wide else whole.at[0]

    def left(block, h, p, act, at=0):
        def copy(wide):
            part = block_of(0, block, h, p, wide)
            return pltpu.make_async_remote_copy(
                src_ref=part, dst_ref=part, send_sem=send_sem.at[0, block, h, p],
                recv_sem=recv_sem.at[block, h, p], device_id={"ctx": z - 1}, device_id_type=MESH)

        pick_size(seen_ahead(block, inner[0] <= z - 1 + at) if inner else None, copy, act)

    def right(block, h, p, act, at=0):
        def copy(wide):
            part = block_of(0, block, h, p, wide)
            return pltpu.make_async_remote_copy(
                src_ref=part, dst_ref=part, send_sem=send_sem.at[1, block, h, p],
                recv_sem=recv_sem.at[block, h, p], device_id={"ctx": z + 1}, device_id_type=MESH)

        pick_size(seen_ahead(block, inner[0] >= z + 1 - at) if inner else None, copy, act)

    def pair(block, h, p, act):
        def copy(wide):
            return pltpu.make_async_remote_copy(
                src_ref=block_of(0, block, h, p, wide), dst_ref=block_of(1, block, h, p, wide),
                send_sem=pair_send.at[block, h, p], recv_sem=pair_recv.at[block, h, p],
                device_id={"sub": 1 - c}, device_id_type=MESH)

        pick_size((block == z) | seen_ahead(block, inner[0] == z) if inner else None, copy, act)

    def start(copy):
        copy.start()

    def sent(copy):
        copy.wait_send()

    def arrived(copy):
        copy.wait_recv()

    def own_copy(p):
        return pltpu.make_async_copy((k_any, v_any)[p], raw.at[p], own_sem.at[p])

    def q_copy(g):
        return pltpu.make_async_copy(q_any.at[:, g], q_raw.at[g], q_sem.at[g])

    for p in range(parts):
        own_copy(p).start()

    barrier = pltpu.get_barrier_semaphore()
    pl.semaphore_signal(barrier, inc=1, device_id={"sub": 1 - c}, device_id_type=MESH)

    @pl.when(has_left)
    def _():
        pl.semaphore_signal(barrier, inc=1, device_id={"ctx": z - 1}, device_id_type=MESH)

    @pl.when(has_right)
    def _():
        pl.semaphore_signal(barrier, inc=1, device_id={"ctx": z + 1}, device_id_type=MESH)

    for g in range(groups):
        q_copy(g).start()

    my_first, my_second = span_ref[2 * z], span_ref[2 * z + 1]
    my_low = jnp.minimum(my_first, my_second)
    flipped = my_first > my_second

    def in_order(first, second):
        return jnp.where(flipped, second, first), jnp.where(flipped, first, second)

    def stage(p, index, carry):
        at = pl.multiple_of(index * PIECE, PIECE)
        first, second = (
            jnp.swapaxes(raw[p, pl.ds(half * span + at, PIECE)], 0, 1) for half in range(2))
        for h in range(heads):
            for half, picked in enumerate(in_order(first[h], second[h])):
                buf[0, z, h, p, half, pl.ds(at, PIECE)] = picked
        return carry

    for p in range(parts):
        own_copy(p).wait()
        lax.fori_loop(0, span // PIECE, functools.partial(stage, p), 0)
        if p == 0:
            pl.semaphore_wait(barrier, 1 + jnp.where(has_left, 1, 0) + jnp.where(has_right, 1, 0))
        for h, which in [(0, 0)] if p == 0 else [(h, q) for h in range(heads) for q in range(parts)][1:]:
            @pl.when(has_left)
            def _(h=h, which=which):
                left(z, h, which, start)

            @pl.when(has_right)
            def _(h=h, which=which):
                right(z, h, which, start)

            pair(z, h, which, start)

    def weigh(scores, top):
        return jnp.exp2((scores - top) * factor)

    def row_max(s):
        return jnp.max(s, axis=0, keepdims=True)

    def with_ones(v):
        return jnp.concatenate([v.T, jnp.ones((16, span), jnp.bfloat16)], axis=0)

    def mix(w, v):
        r = lax.dot_general(v, w, (((1,), (0,)), ((), ())), preferred_element_type=jnp.float32)
        return r[:width], r[width : width + 1]

    def in_stages(score, soften, gather):
        s = score(0)
        held = None
        for j in range(per_row):
            now, s = s, score(j + 1) if j + 1 < per_row else None
            if held is not None:
                gather(j - 1, *held)
            held = soften(j, *now)
        gather(per_row - 1, *held)

    def load_queries(g):
        first = q_raw[g, :span].reshape(per_row, span, width)
        second = q_raw[g, span:].reshape(per_row, span, width)
        for half, picked in enumerate(in_order(first, second)):
            q_ref[g, half] = picked

    def write_out(g, low, high):
        first, second = jnp.where(flipped, high, low), jnp.where(flipped, low, high)
        for i, rows_of in enumerate((first, second)):
            out_ref[i * span : (i + 1) * span, g] = rows_of.T.reshape(span, per_row, width)

    def finish(g):
        write_out(g, *((acc[half, g] * (1.0 / total[half, g])).astype(jnp.bfloat16) for half in range(2)))

    def own_head(k, v, g):
        load_queries(g)
        k_at = lax.broadcasted_iota(jnp.int32, (span, span), 0)
        q_at = lax.broadcasted_iota(jnp.int32, (span, span), 1)
        v_low, v_high = with_ones(v[0]), with_ones(v[1])

        def score(j):
            return scores_of(k[0], q_ref[g, 0, j]), scores_of(k[0], q_ref[g, 1, j]), scores_of(k[1], q_ref[g, 1, j])

        def soften(j, s, s1, s2):
            cols = slice(j * span, (j + 1) * span)
            visible = k_at <= (q_at + j * span) // per_row
            s = jnp.where(visible, s, HIDDEN)
            s2 = jnp.where(visible, s2, HIDDEN)
            top = row_max(s)
            w = weigh(s, top).astype(jnp.bfloat16)
            peak[0, g, :, cols] = top
            top = jnp.maximum(row_max(s1), row_max(s2))
            peak[1, g, :, cols] = top
            return w, weigh(s1, top).astype(jnp.bfloat16), weigh(s2, top).astype(jnp.bfloat16)

        def gather(j, w, w1, w2):
            cols = slice(j * span, (j + 1) * span)
            acc[0, g, :, cols], total[0, g, :, cols] = mix(w, v_low)
            o1, sum1 = mix(w1, v_low)
            o2, sum2 = mix(w2, v_high)
            acc[1, g, :, cols] = o1 + o2
            total[1, g, :, cols] = sum1 + sum2

        in_stages(score, soften, gather)

    def below_of(block):
        return jnp.minimum(span_ref[2 * block], span_ref[2 * block + 1]) < my_low

    def other_head(k, v, block, g, slot):
        below = below_of(block)

        def score(j):
            k_low, k_pick = k[0], jnp.where(below, k[0], k[1])
            q_pick = jnp.where(below, q_ref[g, 0, j], q_ref[g, 1, j])
            return scores_of(k_low, q_ref[g, 1, j]), scores_of(k_pick, q_pick)

        def soften(j, s1, s2):
            cols = slice(j * span, (j + 1) * span)
            top1, top2 = row_max(s1), row_max(s2)
            old_low, old_high = peak[0, g, :, cols], peak[1, g, :, cols]
            new_low = jnp.where(below, jnp.maximum(old_low, top2), old_low)
            new_high = jnp.maximum(old_high, jnp.where(below, top1, jnp.maximum(top1, top2)))
            w1 = weigh(s1, new_high).astype(jnp.bfloat16)
            w2 = weigh(s2, jnp.where(below, new_low, new_high)).astype(jnp.bfloat16)
            peak[0, g, :, cols] = new_low
            peak[1, g, :, cols] = new_high
            return w1, w2, weigh(old_low, new_low), weigh(old_high, new_high)

        def hold(j, w1, w2, r_low, r_high):
            cols = slice(j * span, (j + 1) * span)
            weights[slot, 0, :, cols] = w1
            weights[slot, 1, :, cols] = w2
            rescale[slot, 0, :, cols] = r_low
            rescale[slot, 1, :, cols] = r_high

        def added(j, w1, w2, r_low, r_high):
            cols = slice(j * span, (j + 1) * span)
            o1, sum1 = mix(w1, v_low)
            o2, sum2 = mix(w2, v_pick)
            low = acc[0, g, :, cols] * r_low + jnp.where(below, o2, 0.0)
            high = acc[1, g, :, cols] * r_high + jnp.where(below, o1, o1 + o2)
            low_sum = total[0, g, :, cols] * r_low + jnp.where(below, sum2, 0.0)
            high_sum = total[1, g, :, cols] * r_high + jnp.where(below, sum1, sum1 + sum2)
            return low, high, low_sum, high_sum

        def gather(j, *held):
            cols = slice(j * span, (j + 1) * span)
            acc[0, g, :, cols], acc[1, g, :, cols], total[0, g, :, cols], total[1, g, :, cols] = added(j, *held)

        if v is None:
            in_stages(score, soften, hold)
            return
        v_low, v_pick = with_ones(v[0]), with_ones(jnp.where(below, v[0], v[1]))
        if k is not None:
            in_stages(score, soften, gather)
            return
        lows, highs = [], []
        for j in range(per_row):
            cols = slice(j * span, (j + 1) * span)
            low, high, low_sum, high_sum = added(
                j, weights[slot, 0, :, cols], weights[slot, 1, :, cols],
                rescale[slot, 0, :, cols], rescale[slot, 1, :, cols])
            lows.append((low * (1.0 / low_sum)).astype(jnp.bfloat16))
            highs.append((high * (1.0 / high_sum)).astype(jnp.bfloat16))
        write_out(g, jnp.concatenate(lows, axis=1), jnp.concatenate(highs, axis=1))

    for g in range(groups):
        q_copy(g).wait()

    def own_step(index, carry):
        side, h = index // heads, index % heads

        @pl.when(side == 1)
        def _():
            for p in range(parts):
                pair(z, h, p, arrived)

        own_head(buf[side, z, h, 0], buf[side, z, h, 1], jnp.where(side == 0, c, 1 - c) * heads + h)
        return carry

    lax.fori_loop(0, 2 * heads, own_step, 0)

    def step(merged, index, carry):
        hop = index // heads + 1
        h = index % heads
        left_block, right_block = z - hop, z + hop

        def relay(p):
            @pl.when(left_block >= 0)
            def _():
                block = left_block
                right(block, h, p, arrived, at=1)

                @pl.when(has_right)
                def _():
                    right(block, h, p, start)

                pair(block, h, p, start)

            @pl.when(right_block < n)
            def _():
                block = right_block
                left(block, h, p, arrived, at=1)

                @pl.when(has_left)
                def _():
                    left(block, h, p, start)

                pair(block, h, p, start)

        def part(uses, which, carry):
            side = which // 2
            block = jnp.where(which % 2 == 0, left_block, right_block)
            g = jnp.where(side == 0, c, 1 - c) * heads + h

            @pl.when((block >= 0) & (block < n))
            def _():
                @pl.when(side == 1)
                def _():
                    for p in uses:
                        pair(block, h, p, arrived)

                k, v = (buf[side, block, h, p] if p in uses else None for p in range(parts))
                other_head(k, v, block, g, which)

            return carry

        relay(0)
        if merged:
            relay(1)
            return lax.fori_loop(0, 4, functools.partial(part, (0, 1)), carry)
        lax.fori_loop(0, 4, functools.partial(part, (0,)), 0)
        relay(1)

        @pl.when(has_left & has_right)
        def _():
            lax.fori_loop(0, 2, lambda side, carry: finish(side * heads + h) or carry, 0)

        return lax.fori_loop(0, 4, functools.partial(part, (1,)), carry)

    lax.fori_loop(0, (n - 2) * heads, functools.partial(step, True), 0)
    lax.fori_loop((n - 2) * heads, (n - 1) * heads, functools.partial(step, False), 0)

    def drain(index, carry):
        block = index // heads
        h = index % heads
        for p in range(parts):
            @pl.when(has_left & (block >= z))
            def _(p=p):
                left(block, h, p, sent)

            @pl.when(has_right & (block <= z))
            def _(p=p):
                right(block, h, p, sent)

            pair(block, h, p, sent)
        return carry

    lax.fori_loop(0, n * heads, drain, 0)


def last_holder(span_ref, holder_ref):
    n = span_ref.shape[0] // 2
    holder = 0
    for i in range(1, n):
        holder = jnp.where(jnp.maximum(span_ref[2 * i], span_ref[2 * i + 1]) == 2 * n - 1, i, holder)
    holder_ref[0] = holder


def attend(n, inner, number, queries, keys, values, span_order):
    rows, groups, per_group, width = queries.shape
    heads = keys.shape[1]
    span = rows // 2
    q_rows = span * per_group
    in_hbm = pl.BlockSpec(memory_space=pltpu.HBM)
    return pl.pallas_call(
        functools.partial(kernel, n, inner),
        out_shape=jax.ShapeDtypeStruct(queries.shape, jnp.bfloat16),
        in_specs=[pl.BlockSpec(memory_space=pltpu.SMEM), in_hbm, in_hbm, in_hbm],
        out_specs=pl.BlockSpec(memory_space=pltpu.VMEM),
        scratch_shapes=[
            pltpu.VMEM((2, rows, heads, width), jnp.bfloat16),
            pltpu.VMEM((groups, rows, per_group, width), jnp.bfloat16),
            pltpu.VMEM((groups, 2, per_group, span, width), jnp.bfloat16),
            pltpu.VMEM((2, n, heads, 2, 2, span, width), jnp.bfloat16),
            pltpu.VMEM((2, groups, width, q_rows), jnp.float32),
            pltpu.VMEM((2, groups, 1, q_rows), jnp.float32),
            pltpu.VMEM((2, groups, 1, q_rows), jnp.float32),
            pltpu.VMEM((4, 2, span, q_rows), jnp.bfloat16),
            pltpu.VMEM((4, 2, 1, q_rows), jnp.float32),
            pltpu.SemaphoreType.DMA((2, n, heads, 2)),
            pltpu.SemaphoreType.DMA((n, heads, 2)),
            pltpu.SemaphoreType.DMA((n, heads, 2)),
            pltpu.SemaphoreType.DMA((n, heads, 2)),
            pltpu.SemaphoreType.DMA((2,)),
            pltpu.SemaphoreType.DMA((groups,)),
        ],
        compiler_params=pltpu.CompilerParams(
            collective_id=number, has_side_effects=True, vmem_limit_bytes=48 * 1024 * 1024),
    )(*(pltpu.with_memory_space_constraint(a, pltpu.HBM) for a in (span_order, queries, keys, values)))


def on_device(n, queries, keys, values, span_order):
    args = (queries, keys, values, span_order)
    if n > MOST_LAYOUTS:
        return attend(n, (), 0, *args)
    in_smem = pl.BlockSpec(memory_space=pltpu.SMEM)
    holder = pl.pallas_call(
        last_holder, out_shape=jax.ShapeDtypeStruct((1,), jnp.int32), in_specs=[in_smem], out_specs=in_smem)(span_order)
    return lax.switch(holder[0], [functools.partial(attend, n, (i,), i) for i in range(n)], *args)


def solution(mesh):
    return jax.shard_map(
        functools.partial(on_device, mesh.shape["ctx"]),
        mesh=mesh,
        in_specs=(
            P(("groups", "ctx"), "head", "sub", None),
            P(("groups", "ctx"), ("head", "sub"), None),
            P(("groups", "ctx"), ("head", "sub"), None),
            P(),
        ),
        out_specs=P(("groups", "ctx"), "head", "sub", None),
        check_vma=False,
    )
```
